32 devices in a mesh: row: 16 (over z, y, core), col: 2 (over x).
Axes of the slice: x: 2, y: 2, z: 4, core: 2. Of those that a mesh axis runs over, the one named last changes fastest.
Arguments:
- states: bfloat16 [768, 8192], P(None, 'col'), may hold values from -6 to 6
- norm_gain: float32 [8192], P('col'), may hold values from 0.25 to 1.75
- gate_weight: bfloat16 [8192, 28672], P('col', 'row'), may hold values from -0.0625 to 0.0625
- up_weight: bfloat16 [8192, 28672], P('col', 'row'), may hold values from -0.0625 to 0.0625
Outputs:
- near_tiles: float32 [16, 8, 1792, 1792], P('row', 'col')
- far_tiles: float32 [16, 1792, 1792], P('row', 'col')
The draws below stay inside these ranges and needn't reach their ends.
All inputs are finite; a program needn't handle non-finite values.
Results may differ from the reference program's by a relative error of at most 0.0071.
Values may be sent and summed in bfloat16 or wider, within the bound.
A program may use at most 192 MiB of HBM per device.

```python
import jax
import jax.numpy as jnp
from jax import lax

D = 8192
FF = 28672
TOKENS = 768
BLOCK = 1792
N_ROW = 16


def block_levels(stream_key, dims, cuts, smallest, high):
    factor_of = 1.0
    for dim, shards_of in cuts:
        draws = jax.random.uniform(jax.random.fold_in(jax.random.fold_in(stream_key, 6), dim), (shards_of,), jnp.float32, smallest / len(cuts), high / len(cuts))
        factor_of = factor_of * jnp.repeat(jnp.exp(draws), dims[dim] // shards_of).reshape((-1,) + (1,) * (len(dims) - 1 - dim))
    return factor_of


def noise(own_key, dims, spread, bound, split=(), kind=jnp.bfloat16):
    values = jax.random.normal(own_key, dims, jnp.float32) * spread
    if len(split) > 0:
        values = block_levels(own_key, dims, split, -0.22, 0.18) * values
    return jnp.clip(values, min=-bound, max=bound).astype(kind)


def setup_inputs(seed: int = 0) -> dict:
    arg_keys = jax.random.split(jax.random.key(seed), 5)
    states = noise(arg_keys[0], (TOKENS, D), 1.0, 6.0, ((1, 2),))
    norm_gain = jnp.clip(1.0 + 0.15 * jax.random.normal(arg_keys[1], (D,), jnp.float32), 0.25, 1.75)
    gate_weight = noise(arg_keys[2], (D, FF), D ** -0.5, 0.0625, ((0, 2), (1, 16)))
    up_weight = noise(arg_keys[3], (D, FF), D ** -0.5, 0.0625, ((0, 2), (1, 16)))
    return dict(states=states, norm_gain=norm_gain, gate_weight=gate_weight, up_weight=up_weight)


def reference(states, norm_gain, gate_weight, up_weight):
    wide = states.astype(jnp.float32)
    inverse = lax.rsqrt(lax.optimization_barrier(jnp.mean(wide * wide, axis=1)) + 1e-05)
    normed = (wide * inverse[:, None] * norm_gain[None, :]).astype(jnp.bfloat16)
    gate = jnp.dot(normed, gate_weight, preferred_element_type=jnp.float32)
    up = jnp.dot(normed, up_weight, preferred_element_type=jnp.float32)
    keys = (jax.nn.silu(gate) * up).astype(jnp.bfloat16)
    count = keys.shape[0]
    blocks = keys.astype(jnp.float32).reshape(count, N_ROW, BLOCK)
    half = N_ROW // 2

    def one_block(index):
        own = lax.dynamic_index_in_dim(blocks, index, 1, keepdims=False)
        rolled = jnp.roll(blocks, -index, axis=1)
        near = jnp.einsum('tk,tmj->mkj', own, rolled[:, :half], precision=lax.Precision.HIGHEST) / count
        far = jnp.einsum('tk,tj->kj', own, rolled[:, half], precision=lax.Precision.HIGHEST) / count
        return (near, far)
    near_tiles, far_tiles = lax.map(one_block, jnp.arange(N_ROW, dtype=jnp.int32))
    return (near_tiles, far_tiles)
```

```python
import functools

import jax
import jax.numpy as jnp
from jax import lax
from jax.experimental import pallas as pl
from jax.experimental.pallas import tpu as pltpu
from jax.sharding import PartitionSpec as P

LANES = 128
SLOTS = 4
PARTS = 1
EARLY = 0
CROSS = 8
MESH = pl.DeviceIdType.MESH
(SUM, PAIR, NEXT_OWN, NEXT_OTHER, FAR_OWN, FAR_OTHER, RELAY_OWN, RELAY_OTHER,
 LAST_OWN, LAST_OTHER, SIDE_OWN, SIDE_OTHER, CORE_ODD, CORE_TOP, ACROSS, FAR_ALL, RELAY_ALL) = range(17)
OWN, STEP, OPPOSITE, BASE1, BASE2, BASE3 = range(6)


def passed_along(shard, axis, by):
    devices = lax.axis_size(axis)
    return lax.ppermute(shard, axis, [(i, (i + by) % devices) for i in range(devices)])


def cross(left, right):
    return lax.dot_general(
        left, right, (((0,), (0,)), ((), ())), preferred_element_type=jnp.float32
    )


def gather_kernel(n_row, step, features, x_hbm, gain_ref, gate_hbm, up_hbm, kept, x_ref, wbuf, partial, sent,
                  got, mine, squares, squares_got, x_sem, w_sem, local_sem, norm_sem, send_sem, recv_sem):
    row = lax.axis_index("row")
    col = lax.axis_index("col")
    core = lax.rem(row, 2)
    y = lax.rem(lax.div(row, 2), 2)
    items, few, wide = sent.shape
    count, depth = x_ref.shape
    strips = squares.shape[0]
    cut = wide // 2
    half = count // 2
    chunks = items // PARTS
    own_rows = pl.ds(pl.multiple_of(col * half, half), half)
    other_rows = pl.ds(pl.multiple_of((1 - col) * half, half), half)
    cross = few * CROSS // 64 * 4

    pair = (row, 1 - col)
    level = lax.div(row, step)
    below = (lax.rem(row + n_row - step, n_row), col)
    above = (lax.rem(row + step, n_row), col)
    two_off = (lax.rem(row + 2 * step, n_row), col)
    side = (row + 2 - 4 * y, col)
    twin = (row + 1 - 2 * core, col)

    def weights(j, slot):
        cols = pl.ds(pl.multiple_of(j * cut, cut), cut)
        return (
            pltpu.make_async_copy(gate_hbm.at[:, cols], wbuf.at[slot, :, pl.ds(0, cut)], w_sem.at[slot, 0]),
            pltpu.make_async_copy(up_hbm.at[:, cols], wbuf.at[slot, :, pl.ds(cut, cut)], w_sem.at[slot, 1]),
        )

    def strip(r):
        return pl.ds(pl.multiple_of(r * LANES, LANES), LANES)

    def states(r):
        return pltpu.make_async_copy(x_hbm.at[strip(r)], x_ref.at[strip(r)], x_sem.at[r])

    def part(slot, i, side=None, skip=0, rows=None):
        start = lax.rem(i, PARTS) * 2 * few
        if side is None:
            rows = 2 * few
        else:
            start = start + side * few + skip
            rows = few if rows is None else rows
        return kept.at[slot, lax.div(i, PARTS), pl.ds(pl.multiple_of(start, 16), rows)]

    def remote(kind, i, src, dst, to):
        return pltpu.make_async_remote_copy(
            src_ref=src, dst_ref=dst, send_sem=send_sem.at[kind, i], recv_sem=recv_sem.at[kind, i],
            device_id=to, device_id_type=MESH,
        )

    def copies(i):
        own = functools.partial(part, i=i, side=col)
        other = functools.partial(part, i=i, side=1 - col)
        fewer = functools.partial(part, i=i, side=1 - col, rows=few - cross)
        crossing = part(OPPOSITE, i, col, few - cross, cross)
        made = {
            SUM: (sent.at[i], got.at[i], pair),
            PAIR: (mine.at[i], own(OWN), pair),
            NEXT_OWN: (mine.at[i], own(STEP), below),
            NEXT_OTHER: (other(OWN), other(STEP), below),
            FAR_OWN: (mine.at[i], own(OPPOSITE), two_off),
            FAR_OTHER: (fewer(OWN), fewer(OPPOSITE), two_off),
            RELAY_OWN: (own(STEP), own(OPPOSITE), below),
            RELAY_OTHER: (fewer(STEP), fewer(OPPOSITE), below),
            LAST_OWN: (own(OPPOSITE), own(STEP), above),
            LAST_OTHER: (other(OPPOSITE), other(STEP), above),
            SIDE_OWN: (own(col + 1 - y), own(BASE2), side),
            SIDE_OTHER: (other(col + 1 - y), other(BASE2), side),
            FAR_ALL: (other(OWN), other(OPPOSITE), two_off),
            RELAY_ALL: (other(STEP), other(OPPOSITE), below),
            CORE_ODD: (part(BASE2 * (1 - core) + col * core, i), part(BASE1, i), twin),
            CORE_TOP: (part((col + 1) * (1 - core) + BASE2 * core, i), part(BASE3, i), twin),
            ACROSS: (crossing, crossing, pair),
        }
        return {kind: functools.partial(remote, kind, i, *ends) for kind, ends in made.items()}

    def local(i):
        return pltpu.make_async_copy(mine.at[i], part(OWN, i, col), local_sem.at[i])

    for r in range(strips):
        states(r).start()
    for copy in weights(0, 0):
        copy.start()
    barrier = pltpu.get_barrier_semaphore()
    for device in (pair, below, above, two_off, side, twin):
        pl.semaphore_signal(barrier, inc=1, device_id=device, device_id_type=MESH)

    @pl.loop(0, strips)
    def _(r):
        states(r).wait()
        total = jnp.zeros((LANES, LANES), jnp.float32)
        for g in range(0, depth, LANES):
            v = x_ref[strip(r), g:g + LANES].astype(jnp.float32)
            total += v * v
        squares[r] = jnp.broadcast_to(jnp.sum(total.T, axis=0, keepdims=True), squares.shape[1:])

    pl.semaphore_wait(barrier, 6)
    swap = pltpu.make_async_remote_copy(
        src_ref=squares, dst_ref=squares_got, send_sem=norm_sem.at[0], recv_sem=norm_sem.at[1],
        device_id=pair, device_id_type=MESH,
    )
    swap.start()
    swap.wait()

    @pl.loop(0, strips)
    def _(r):
        total = squares[r] + squares_got[r]
        inverse = lax.rsqrt(jnp.broadcast_to(total[:1], (LANES, LANES)).T / features + 1e-05)
        for g in range(0, depth, LANES):
            v = x_ref[strip(r), g:g + LANES].astype(jnp.float32)
            x_ref[strip(r), g:g + LANES] = (v * inverse * gain_ref[:, g:g + LANES]).astype(jnp.bfloat16)

    def stage(t, lag, act):
        i = t - lag

        @pl.when(jnp.logical_and(i >= 0, i < items))
        def _():
            act(i, copies(i))

    def multiply(i, copy):
        j = lax.div(i, PARTS)
        slot = lax.rem(j, 2)

        @pl.when(lax.rem(i, PARTS) == 0)
        def _():
            for w in weights(j, slot):
                w.wait()

            @pl.when(j + 1 < chunks)
            def _():
                for w in weights(j + 1, 1 - slot):
                    w.start()

            theirs = jnp.dot(
                x_ref[other_rows, :], wbuf[slot], preferred_element_type=jnp.float32
            ).astype(jnp.bfloat16)
            for p in range(PARTS):
                sent[i + p] = theirs[p * few:(p + 1) * few]
            copy[SUM]().start()
            ours = jnp.dot(x_ref[own_rows, :], wbuf[slot], preferred_element_type=jnp.float32)
            for p in range(PARTS):
                partial[slot, p] = ours[p * few:(p + 1) * few]

        pl.when(lax.rem(i, PARTS) > 0)(lambda: copy[SUM]().start())

    def activate(i, copy):
        copy[SUM]().wait_recv()
        total = partial[lax.rem(lax.div(i, PARTS), 2), lax.rem(i, PARTS)] + got[i].astype(jnp.float32)
        gate = total[:, :cut]
        mine[i] = (gate / (1.0 + jnp.exp(-gate)) * total[:, cut:]).astype(jnp.bfloat16)
        copy[PAIR]().start()
        start(copy, FAR_OWN)
        start(copy, NEXT_OWN)
        local(i).start()

    senders = {
        NEXT_OWN: level >= 1, NEXT_OTHER: level >= 1,
        FAR_OWN: level <= 1, FAR_OTHER: level <= 1, FAR_ALL: level <= 1,
        RELAY_OWN: jnp.logical_or(level == 1, level == 2),
        RELAY_OTHER: jnp.logical_or(level == 1, level == 2), RELAY_ALL: jnp.logical_or(level == 1, level == 2),
        LAST_OWN: level == 2, LAST_OTHER: level == 2,
    }
    receivers = {
        NEXT_OWN: level <= 2, NEXT_OTHER: level <= 2,
        FAR_OWN: level >= 2, FAR_OTHER: level >= 2, FAR_ALL: level >= 2,
        RELAY_OWN: level <= 1, RELAY_OTHER: level <= 1, RELAY_ALL: level <= 1,
        LAST_OWN: level == 3, LAST_OTHER: level == 3,
    }

    early = {FAR_ALL, RELAY_ALL}
    late = {FAR_OTHER, RELAY_OTHER, ACROSS}

    def holds(role, kind, i):
        if kind in early:
            return jnp.logical_and(role, i < EARLY)
        return jnp.logical_and(role, i >= EARLY) if kind in late else role

    def start(copy, kind, i=None):
        pl.when(holds(senders[kind], kind, i))(lambda: copy[kind]().start())

    def receive(copy, kind, i=None):
        pl.when(holds(receivers[kind], kind, i))(lambda: copy[kind]().wait_recv())

    def across(copy, i, here):
        pl.when(holds(here, ACROSS, i))(lambda: copy[ACROSS]().start())

    def crossed(copy, i, here):
        pl.when(holds(here, ACROSS, i))(lambda: copy[ACROSS]().wait_recv())

    def paired(i, copy):
        copy[PAIR]().wait_recv()
        start(copy, FAR_OTHER, i)
        start(copy, FAR_ALL, i)
        start(copy, NEXT_OTHER)

    def hop_own(i, copy):
        receive(copy, NEXT_OWN)
        start(copy, RELAY_OWN)
        receive(copy, FAR_OWN)
        start(copy, LAST_OWN)
        across(copy, i, level >= 2)

    def hop_other(i, copy):
        receive(copy, NEXT_OTHER)
        start(copy, RELAY_OTHER, i)
        start(copy, RELAY_ALL, i)

    def onward(i, copy):
        receive(copy, FAR_OTHER, i)
        receive(copy, FAR_ALL, i)
        crossed(copy, i, level >= 2)
        start(copy, LAST_OTHER)
        receive(copy, RELAY_OWN)
        across(copy, i, level <= 1)
        local(i).wait()
        receive(copy, LAST_OWN)
        copy[SIDE_OWN]().start()

    def sideways(i, copy):
        receive(copy, RELAY_OTHER, i)
        receive(copy, RELAY_ALL, i)
        crossed(copy, i, level <= 1)
        receive(copy, LAST_OTHER)
        copy[SIDE_OTHER]().start()

    def within(i, copy):
        copy[SIDE_OWN]().wait_recv()
        copy[SIDE_OTHER]().wait_recv()
        copy[CORE_ODD]().start()
        copy[CORE_TOP]().start()

    def arrive(i, copy):
        copy[CORE_ODD]().wait_recv()
        copy[CORE_TOP]().wait_recv()
        for kind in copy:
            held = holds(senders.get(kind, level >= 0), kind, i)
            pl.when(held)(lambda kind=kind: copy[kind]().wait_send())

    @pl.loop(0, items + 7)
    def _(t):
        stage(t, 0, multiply)
        stage(t, 1, activate)
        stage(t, 2, paired)
        stage(t, 2, hop_own)
        stage(t, 3, hop_other)
        stage(t, 4, onward)
        stage(t, 5, sideways)
        stage(t, 6, within)
        stage(t, 7, arrive)


def gather_keys(n_row, step, features, states, norm_gain, gate_weight, up_weight):
    count, depth = states.shape
    width = gate_weight.shape[1]
    cut = LANES
    items = width // cut * PARTS
    few = count // 2 // PARTS
    strips = count // LANES
    return pl.pallas_call(
        functools.partial(gather_kernel, n_row, step, features),
        out_shape=jax.ShapeDtypeStruct((6, width // LANES, count, LANES), jnp.bfloat16),
        in_specs=[
            pl.BlockSpec(memory_space=pl.ANY),
            pl.BlockSpec(memory_space=pltpu.VMEM),
            pl.BlockSpec(memory_space=pl.ANY),
            pl.BlockSpec(memory_space=pl.ANY),
        ],
        out_specs=pl.BlockSpec(memory_space=pl.ANY),
        scratch_shapes=[
            pltpu.VMEM((count, depth), jnp.bfloat16),
            pltpu.VMEM((2, depth, 2 * cut), jnp.bfloat16),
            pltpu.VMEM((2, PARTS, few, 2 * cut), jnp.float32),
            pltpu.VMEM((items, few, 2 * cut), jnp.bfloat16),
            pltpu.VMEM((items, few, 2 * cut), jnp.bfloat16),
            pltpu.VMEM((items, few, LANES), jnp.bfloat16),
            pltpu.VMEM((strips, 8, LANES), jnp.float32),
            pltpu.VMEM((strips, 8, LANES), jnp.float32),
            pltpu.SemaphoreType.DMA((strips,)),
            pltpu.SemaphoreType.DMA((2, 2)),
            pltpu.SemaphoreType.DMA((items,)),
            pltpu.SemaphoreType.DMA((2,)),
            pltpu.SemaphoreType.DMA((17, items)),
            pltpu.SemaphoreType.DMA((17, items)),
        ],
        compiler_params=pltpu.CompilerParams(
            collective_id=0, has_side_effects=True, vmem_limit_bytes=56 * 2**20
        ),
        name="gather_keys",
    )(states, norm_gain.reshape(1, depth), gate_weight, up_weight)


def tiles_kernel(scale, kept, near_hbm, far_hbm, left, right, filled, left_sem, right_sem, out_sem):
    col = lax.axis_index("col")
    blocks, count = left.shape[0], left.shape[1]
    slab = far_hbm.shape[1]
    per_col = near_hbm.shape[1]
    pairs = blocks // 2
    pair = 2 * LANES
    slots = filled.shape[0]
    nears = per_col * pairs

    def fetch(m):
        block = jnp.where(m == 0, col, jnp.where(m == per_col, OPPOSITE, OPPOSITE + m))
        slot = lax.rem(m, 2)
        return pltpu.make_async_copy(kept.at[block], right.at[slot], right_sem.at[slot])

    def near_out(n):
        slot = lax.rem(n, slots)
        cols = pl.ds(pl.multiple_of(lax.rem(n, pairs) * pair, pair), pair)
        return pltpu.make_async_copy(filled.at[slot], near_hbm.at[0, lax.div(n, pairs), :, cols], out_sem.at[slot])

    def far_out(n):
        slot = lax.rem(n, slots)
        cols = pl.ds(pl.multiple_of((n - nears) * pair, pair), pair)
        return pltpu.make_async_copy(filled.at[slot, pl.ds(0, slab)], far_hbm.at[0, :, cols], out_sem.at[slot])

    def product(lefts, m, b):
        slot = lax.rem(m, 2)
        both = jnp.concatenate([right[slot, 2 * b], right[slot, 2 * b + 1]], axis=1)
        return lax.dot_general(
            lefts, both, (((0,), (0,)), ((), ())), preferred_element_type=jnp.float32
        ) * scale

    own = pltpu.make_async_copy(kept.at[OWN], left, left_sem.at[0])
    own.start()
    fetch(0).start()
    own.wait()

    @pl.loop(0, nears)
    def _(n):
        m, b = lax.div(n, pairs), lax.rem(n, pairs)

        @pl.when(b == 0)
        def _():
            fetch(m).wait()
            fetch(m + 1).start()

        pl.when(n >= slots)(lambda: near_out(n - slots).wait())
        lefts = jnp.concatenate([left[k] for k in range(blocks)], axis=1)
        filled[lax.rem(n, slots)] = product(lefts, m, b)
        near_out(n).start()

    fetch(per_col).wait()

    @pl.loop(nears, nears + pairs)
    def _(n):
        pl.when(n - slots < nears)(lambda: near_out(n - slots).wait())
        pl.when(n - slots >= nears)(lambda: far_out(n - slots).wait())
        first = col * (blocks // 2)
        lefts = jnp.concatenate([left[first + k] for k in range(blocks // 2)], axis=1)
        filled[lax.rem(n, slots), :slab] = product(lefts, per_col, n - nears)
        far_out(n).start()

    for n in range(nears + pairs - slots, nears + pairs):
        far_out(n).wait()


def tiles(kept, per_col, scale):
    _, blocks, count, _ = kept.shape
    width = blocks * LANES
    slab = width // 2
    return pl.pallas_call(
        functools.partial(tiles_kernel, scale),
        in_specs=[pl.BlockSpec(memory_space=pl.ANY)],
        out_specs=[pl.BlockSpec(memory_space=pl.ANY), pl.BlockSpec(memory_space=pl.ANY)],
        out_shape=(
            jax.ShapeDtypeStruct((1, per_col, width, width), jnp.float32),
            jax.ShapeDtypeStruct((1, slab, width), jnp.float32),
        ),
        scratch_shapes=[
            pltpu.VMEM((blocks, count, LANES), jnp.bfloat16),
            pltpu.VMEM((2, blocks, count, LANES), jnp.bfloat16),
            pltpu.VMEM((SLOTS, width, 2 * LANES), jnp.float32),
            pltpu.SemaphoreType.DMA((1,)),
            pltpu.SemaphoreType.DMA((2,)),
            pltpu.SemaphoreType.DMA((SLOTS,)),
        ],
        compiler_params=pltpu.CompilerParams(vmem_limit_bytes=56 * 2**20),
        name="tiles",
    )(kept)


def by_routes(states, norm_gain, gate_weight, up_weight):
    n_row = lax.axis_size("row")
    n_col = lax.axis_size("col")
    per_col = n_row // (2 * n_col)
    features = states.shape[1] * n_col
    kept = gather_keys(n_row, per_col, features, states, norm_gain, gate_weight, up_weight)
    return tiles(kept, per_col, 1.0 / states.shape[0])


def on_device(states, norm_gain, gate_weight, up_weight):
    n_row = lax.axis_size("row")
    n_col = lax.axis_size("col")
    column = lax.axis_index("col")
    width = gate_weight.shape[1]
    count = states.shape[0]
    wide = states.astype(jnp.float32)
    squares = lax.psum(jnp.sum(wide * wide, axis=1), "col")
    inverse = lax.rsqrt(squares / (states.shape[1] * n_col) + 1e-05)
    normed = (wide * inverse[:, None] * norm_gain[None, :]).astype(jnp.bfloat16)
    gate_part = jnp.dot(normed, gate_weight, preferred_element_type=jnp.float32)
    up_part = jnp.dot(normed, up_weight, preferred_element_type=jnp.float32)
    summed = lax.psum_scatter(
        jnp.concatenate([gate_part, up_part], axis=1), "col", scatter_dimension=0, tiled=True
    )
    own_keys = (jax.nn.silu(summed[:, :width]) * summed[:, width:]).astype(jnp.bfloat16)
    keys = lax.all_gather(own_keys, "col", axis=0, tiled=True)
    per_col = n_row // (2 * n_col)
    scale = 1.0 / count
    partner = keys
    for target in range(1, n_col):
        arrived = passed_along(keys, "row", n_row - target * per_col)
        partner = jnp.where(column == target, arrived, partner)
    tiles = [cross(keys, partner) * scale]
    for offset in range(1, per_col):
        partner = passed_along(partner, "row", n_row - 1)
        tiles.append(cross(keys, partner) * scale)
    opposite = passed_along(keys, "row", n_row // 2)
    near_tiles = jnp.stack(tiles, axis=0)[None]
    slab = width // n_col
    own_cols = lax.dynamic_slice_in_dim(keys, column * slab, slab, 1)
    far_tiles = (cross(own_cols, opposite) * scale)[None]
    return (near_tiles, far_tiles)


def fits(mesh, states, gate_weight):
    n_row, n_col = mesh.shape["row"], mesh.shape["col"]
    width = gate_weight.shape[1] // n_row
    return n_col == 2 and n_row == 8 * n_col and width % (4 * LANES) in (0, 2 * LANES) and width // (2 * LANES) >= SLOTS and states.shape[0] % (2 * LANES) == 0


def solution(mesh):
    placed = (P(None, "col"), P("col"), P("col", "row"), P("col", "row"))

    def program(states, norm_gain, gate_weight, up_weight):
        on_each = by_routes if fits(mesh, states, gate_weight) else on_device
        return jax.shard_map(
            on_each,
            mesh=mesh,
            in_specs=placed,
            out_specs=(P("row", "col", None, None), P("row", "col", None)),
            check_vma=False,
        )(states, norm_gain, gate_weight, up_weight)

    return program
```

```python
import functools

import jax
import jax.numpy as jnp
from jax import lax
from jax.experimental import pallas as pl
from jax.experimental.pallas import tpu as pltpu
from jax.sharding import PartitionSpec as P

LANES = 128
SLOTS = 4
PARTS = 1
CROSS = 8
MESH = pl.DeviceIdType.MESH
(SUM, PAIR, NEXT_OWN, NEXT_OTHER, FAR_OWN, FAR_OTHER, RELAY_OWN, RELAY_OTHER,
 LAST_OWN, LAST_OTHER, SIDE_OWN, SIDE_OTHER, CORE_ODD, CORE_TOP, ACROSS) = range(15)
OWN, STEP, OPPOSITE, BASE1, BASE2, BASE3 = range(6)


def passed_along(shard, axis, by):
    devices = lax.axis_size(axis)
    return lax.ppermute(shard, axis, [(i, (i + by) % devices) for i in range(devices)])


def cross(left, right):
    return lax.dot_general(
        left, right, (((0,), (0,)), ((), ())), preferred_element_type=jnp.float32
    )


def gather_kernel(n_row, step, features, x_hbm, gain_ref, gate_hbm, up_hbm, kept, x_ref, wbuf, partial, sent,
                  got, mine, squares, squares_got, x_sem, w_sem, local_sem, norm_sem, send_sem, recv_sem):
    row = lax.axis_index("row")
    col = lax.axis_index("col")
    core = lax.rem(row, 2)
    y = lax.rem(lax.div(row, 2), 2)
    items, few, wide = sent.shape
    count, depth = x_ref.shape
    strips = squares.shape[0]
    cut = wide // 2
    half = count // 2
    chunks = items // PARTS
    own_rows = pl.ds(pl.multiple_of(col * half, half), half)
    other_rows = pl.ds(pl.multiple_of((1 - col) * half, half), half)
    cross = few * CROSS // 64 * 4

    pair = (row, 1 - col)
    level = lax.div(row, step)
    below = (lax.rem(row + n_row - step, n_row), col)
    above = (lax.rem(row + step, n_row), col)
    two_off = (lax.rem(row + 2 * step, n_row), col)
    side = (row + 2 - 4 * y, col)
    twin = (row + 1 - 2 * core, col)

    def weights(j, slot):
        cols = pl.ds(pl.multiple_of(j * cut, cut), cut)
        return (
            pltpu.make_async_copy(gate_hbm.at[:, cols], wbuf.at[slot, :, pl.ds(0, cut)], w_sem.at[slot, 0]),
            pltpu.make_async_copy(up_hbm.at[:, cols], wbuf.at[slot, :, pl.ds(cut, cut)], w_sem.at[slot, 1]),
        )

    def strip(r):
        return pl.ds(pl.multiple_of(r * LANES, LANES), LANES)

    def states(r):
        return pltpu.make_async_copy(x_hbm.at[strip(r)], x_ref.at[strip(r)], x_sem.at[r])

    def part(slot, i, side=None, skip=0, rows=None):
        start = lax.rem(i, PARTS) * 2 * few
        if side is None:
            rows = 2 * few
        else:
            start = start + side * few + skip
            rows = few if rows is None else rows
        return kept.at[slot, lax.div(i, PARTS), pl.ds(pl.multiple_of(start, 16), rows)]

    def remote(kind, i, src, dst, to):
        return pltpu.make_async_remote_copy(
            src_ref=src, dst_ref=dst, send_sem=send_sem.at[kind, i], recv_sem=recv_sem.at[kind, i],
            device_id=to, device_id_type=MESH,
        )

    def copies(i):
        own = functools.partial(part, i=i, side=col)
        other = functools.partial(part, i=i, side=1 - col)
        fewer = functools.partial(part, i=i, side=1 - col, rows=few - cross)
        crossing = part(OPPOSITE, i, col, few - cross, cross)
        made = {
            SUM: (sent.at[i], got.at[i], pair),
            PAIR: (mine.at[i], own(OWN), pair),
            NEXT_OWN: (mine.at[i], own(STEP), below),
            NEXT_OTHER: (other(OWN), other(STEP), below),
            FAR_OWN: (mine.at[i], own(OPPOSITE), two_off),
            FAR_OTHER: (fewer(OWN), fewer(OPPOSITE), two_off),
            RELAY_OWN: (own(STEP), own(OPPOSITE), below),
            RELAY_OTHER: (fewer(STEP), fewer(OPPOSITE), below),
            LAST_OWN: (own(OPPOSITE), own(STEP), above),
            LAST_OTHER: (other(OPPOSITE), other(STEP), above),
            SIDE_OWN: (own(col + 1 - y), own(BASE2), side),
            SIDE_OTHER: (other(col + 1 - y), other(BASE2), side),
            CORE_ODD: (part(BASE2 * (1 - core) + col * core, i), part(BASE1, i), twin),
            CORE_TOP: (part((col + 1) * (1 - core) + BASE2 * core, i), part(BASE3, i), twin),
            ACROSS: (crossing, crossing, pair),
        }
        return {kind: functools.partial(remote, kind, i, *ends) for kind, ends in made.items()}

    def local(i):
        return pltpu.make_async_copy(mine.at[i], part(OWN, i, col), local_sem.at[i])

    for r in range(strips):
        states(r).start()
    for copy in weights(0, 0):
        copy.start()
    barrier = pltpu.get_barrier_semaphore()
    for device in (pair, below, above, two_off, side, twin):
        pl.semaphore_signal(barrier, inc=1, device_id=device, device_id_type=MESH)

    @pl.loop(0, strips)
    def _(r):
        states(r).wait()
        total = jnp.zeros((LANES, LANES), jnp.float32)
        for g in range(0, depth, LANES):
            v = x_ref[strip(r), g:g + LANES].astype(jnp.float32)
            total += v * v
        squares[r] = jnp.broadcast_to(jnp.sum(total.T, axis=0, keepdims=True), squares.shape[1:])

    pl.semaphore_wait(barrier, 6)
    swap = pltpu.make_async_remote_copy(
        src_ref=squares, dst_ref=squares_got, send_sem=norm_sem.at[0], recv_sem=norm_sem.at[1],
        device_id=pair, device_id_type=MESH,
    )
    swap.start()
    swap.wait()

    @pl.loop(0, strips)
    def _(r):
        total = squares[r] + squares_got[r]
        inverse = lax.rsqrt(jnp.broadcast_to(total[:1], (LANES, LANES)).T / features + 1e-05)
        for g in range(0, depth, LANES):
            v = x_ref[strip(r), g:g + LANES].astype(jnp.float32)
            x_ref[strip(r), g:g + LANES] = (v * inverse * gain_ref[:, g:g + LANES]).astype(jnp.bfloat16)

    def stage(t, lag, act):
        i = t - lag

        @pl.when(jnp.logical_and(i >= 0, i < items))
        def _():
            act(i, copies(i))

    def multiply(i, copy):
        j = lax.div(i, PARTS)
        slot = lax.rem(j, 2)

        @pl.when(lax.rem(i, PARTS) == 0)
        def _():
            for w in weights(j, slot):
                w.wait()

            @pl.when(j + 1 < chunks)
            def _():
                for w in weights(j + 1, 1 - slot):
                    w.start()

            theirs = jnp.dot(
                x_ref[other_rows, :], wbuf[slot], preferred_element_type=jnp.float32
            ).astype(jnp.bfloat16)
            for p in range(PARTS):
                sent[i + p] = theirs[p * few:(p + 1) * few]
            copy[SUM]().start()
            ours = jnp.dot(x_ref[own_rows, :], wbuf[slot], preferred_element_type=jnp.float32)
            for p in range(PARTS):
                partial[slot, p] = ours[p * few:(p + 1) * few]

        pl.when(lax.rem(i, PARTS) > 0)(lambda: copy[SUM]().start())

    def activate(i, copy):
        copy[SUM]().wait_recv()
        total = partial[lax.rem(lax.div(i, PARTS), 2), lax.rem(i, PARTS)] + got[i].astype(jnp.float32)
        gate = total[:, :cut]
        mine[i] = (gate / (1.0 + jnp.exp(-gate)) * total[:, cut:]).astype(jnp.bfloat16)
        copy[PAIR]().start()
        start(copy, FAR_OWN)
        start(copy, NEXT_OWN)
        local(i).start()

    senders = {
        NEXT_OWN: level >= 1, NEXT_OTHER: level >= 1,
        FAR_OWN: level <= 1, FAR_OTHER: level <= 1,
        RELAY_OWN: jnp.logical_or(level == 1, level == 2),
        RELAY_OTHER: jnp.logical_or(level == 1, level == 2),
        LAST_OWN: level == 2, LAST_OTHER: level == 2,
    }
    receivers = {
        NEXT_OWN: level <= 2, NEXT_OTHER: level <= 2,
        FAR_OWN: level >= 2, FAR_OTHER: level >= 2,
        RELAY_OWN: level <= 1, RELAY_OTHER: level <= 1,
        LAST_OWN: level == 3, LAST_OTHER: level == 3,
    }

    def start(copy, kind):
        pl.when(senders[kind])(lambda: copy[kind]().start())

    def receive(copy, kind):
        pl.when(receivers[kind])(lambda: copy[kind]().wait_recv())

    def across(copy, here):
        pl.when(here)(lambda: copy[ACROSS]().start())

    def crossed(copy, here):
        pl.when(here)(lambda: copy[ACROSS]().wait_recv())

    def paired(i, copy):
        copy[PAIR]().wait_recv()
        start(copy, FAR_OTHER)
        start(copy, NEXT_OTHER)

    def hop_own(i, copy):
        receive(copy, NEXT_OWN)
        start(copy, RELAY_OWN)
        receive(copy, FAR_OWN)
        start(copy, LAST_OWN)
        across(copy, level >= 2)

    def hop_other(i, copy):
        receive(copy, NEXT_OTHER)
        start(copy, RELAY_OTHER)

    def onward(i, copy):
        receive(copy, FAR_OTHER)
        crossed(copy, level >= 2)
        start(copy, LAST_OTHER)
        receive(copy, RELAY_OWN)
        across(copy, level <= 1)
        local(i).wait()
        receive(copy, LAST_OWN)
        copy[SIDE_OWN]().start()

    def sideways(i, copy):
        receive(copy, RELAY_OTHER)
        crossed(copy, level <= 1)
        receive(copy, LAST_OTHER)
        copy[SIDE_OTHER]().start()

    def within(i, copy):
        copy[SIDE_OWN]().wait_recv()
        copy[SIDE_OTHER]().wait_recv()
        copy[CORE_ODD]().start()
        copy[CORE_TOP]().start()

    def arrive(i, copy):
        copy[CORE_ODD]().wait_recv()
        copy[CORE_TOP]().wait_recv()
        for kind in copy:
            if kind in senders:
                pl.when(senders[kind])(lambda kind=kind: copy[kind]().wait_send())
            else:
                copy[kind]().wait_send()

    @pl.loop(0, items + 7)
    def _(t):
        stage(t, 0, multiply)
        stage(t, 1, activate)
        stage(t, 2, paired)
        stage(t, 2, hop_own)
        stage(t, 3, hop_other)
        stage(t, 4, onward)
        stage(t, 5, sideways)
        stage(t, 6, within)
        stage(t, 7, arrive)


def gather_keys(n_row, step, features, states, norm_gain, gate_weight, up_weight):
    count, depth = states.shape
    width = gate_weight.shape[1]
    cut = LANES
    items = width // cut * PARTS
    few = count // 2 // PARTS
    strips = count // LANES
    return pl.pallas_call(
        functools.partial(gather_kernel, n_row, step, features),
        out_shape=jax.ShapeDtypeStruct((6, width // LANES, count, LANES), jnp.bfloat16),
        in_specs=[
            pl.BlockSpec(memory_space=pl.ANY),
            pl.BlockSpec(memory_space=pltpu.VMEM),
            pl.BlockSpec(memory_space=pl.ANY),
            pl.BlockSpec(memory_space=pl.ANY),
        ],
        out_specs=pl.BlockSpec(memory_space=pl.ANY),
        scratch_shapes=[
            pltpu.VMEM((count, depth), jnp.bfloat16),
            pltpu.VMEM((2, depth, 2 * cut), jnp.bfloat16),
            pltpu.VMEM((2, PARTS, few, 2 * cut), jnp.float32),
            pltpu.VMEM((items, few, 2 * cut), jnp.bfloat16),
            pltpu.VMEM((items, few, 2 * cut), jnp.bfloat16),
            pltpu.VMEM((items, few, LANES), jnp.bfloat16),
            pltpu.VMEM((strips, 8, LANES), jnp.float32),
            pltpu.VMEM((strips, 8, LANES), jnp.float32),
            pltpu.SemaphoreType.DMA((strips,)),
            pltpu.SemaphoreType.DMA((2, 2)),
            pltpu.SemaphoreType.DMA((items,)),
            pltpu.SemaphoreType.DMA((2,)),
            pltpu.SemaphoreType.DMA((15, items)),
            pltpu.SemaphoreType.DMA((15, items)),
        ],
        compiler_params=pltpu.CompilerParams(
            collective_id=0, has_side_effects=True, vmem_limit_bytes=56 * 2**20
        ),
        name="gather_keys",
    )(states, norm_gain.reshape(1, depth), gate_weight, up_weight)


def tiles_kernel(scale, kept, near_hbm, far_hbm, left, turned, right, filled, left_sem, right_sem, out_sem):
    col = lax.axis_index("col")
    blocks, count = left.shape[0], left.shape[1]
    slab = far_hbm.shape[1]
    per_col = near_hbm.shape[1]
    pairs = blocks // 2
    pair = 2 * LANES
    slots = filled.shape[0]
    nears = per_col * pairs

    def fetch(m):
        block = jnp.where(m == 0, col, jnp.where(m == per_col, OPPOSITE, OPPOSITE + m))
        slot = lax.rem(m, 2)
        return pltpu.make_async_copy(kept.at[block], right.at[slot], right_sem.at[slot])

    def near_out(n):
        slot = lax.rem(n, slots)
        cols = pl.ds(pl.multiple_of(lax.rem(n, pairs) * pair, pair), pair)
        return pltpu.make_async_copy(filled.at[slot], near_hbm.at[0, lax.div(n, pairs), :, cols], out_sem.at[slot])

    def far_out(n):
        slot = lax.rem(n, slots)
        cols = pl.ds(pl.multiple_of((n - nears) * pair, pair), pair)
        return pltpu.make_async_copy(filled.at[slot, pl.ds(0, slab)], far_hbm.at[0, :, cols], out_sem.at[slot])

    def product(lefts, m, b):
        slot = lax.rem(m, 2)
        both = jnp.concatenate([right[slot, 2 * b], right[slot, 2 * b + 1]], axis=1)
        return jnp.dot(lefts, both, preferred_element_type=jnp.float32) * scale

    own = pltpu.make_async_copy(kept.at[OWN], left, left_sem.at[0])
    own.start()
    fetch(0).start()
    own.wait()
    for k in range(blocks):
        turned[k * LANES:(k + 1) * LANES, :] = left[k].T

    @pl.loop(0, nears)
    def _(n):
        m, b = lax.div(n, pairs), lax.rem(n, pairs)

        @pl.when(b == 0)
        def _():
            fetch(m).wait()
            fetch(m + 1).start()

        pl.when(n >= slots)(lambda: near_out(n - slots).wait())
        filled[lax.rem(n, slots)] = product(turned[...], m, b)
        near_out(n).start()

    fetch(per_col).wait()

    @pl.loop(nears, nears + pairs)
    def _(n):
        pl.when(n - slots < nears)(lambda: near_out(n - slots).wait())
        pl.when(n - slots >= nears)(lambda: far_out(n - slots).wait())
        lefts = turned[pl.ds(pl.multiple_of(col * slab, LANES), slab), :]
        filled[lax.rem(n, slots), :slab] = product(lefts, per_col, n - nears)
        far_out(n).start()

    for n in range(nears + pairs - slots, nears + pairs):
        far_out(n).wait()


def tiles(kept, per_col, scale):
    _, blocks, count, _ = kept.shape
    width = blocks * LANES
    slab = width // 2
    return pl.pallas_call(
        functools.partial(tiles_kernel, scale),
        in_specs=[pl.BlockSpec(memory_space=pl.ANY)],
        out_specs=[pl.BlockSpec(memory_space=pl.ANY), pl.BlockSpec(memory_space=pl.ANY)],
        out_shape=(
            jax.ShapeDtypeStruct((1, per_col, width, width), jnp.float32),
            jax.ShapeDtypeStruct((1, slab, width), jnp.float32),
        ),
        scratch_shapes=[
            pltpu.VMEM((blocks, count, LANES), jnp.bfloat16),
            pltpu.VMEM((width, count), jnp.bfloat16),
            pltpu.VMEM((2, blocks, count, LANES), jnp.bfloat16),
            pltpu.VMEM((SLOTS, width, 2 * LANES), jnp.float32),
            pltpu.SemaphoreType.DMA((1,)),
            pltpu.SemaphoreType.DMA((2,)),
            pltpu.SemaphoreType.DMA((SLOTS,)),
        ],
        compiler_params=pltpu.CompilerParams(vmem_limit_bytes=56 * 2**20),
        name="tiles",
    )(kept)


def by_routes(states, norm_gain, gate_weight, up_weight):
    n_row = lax.axis_size("row")
    n_col = lax.axis_size("col")
    per_col = n_row // (2 * n_col)
    features = states.shape[1] * n_col
    kept = gather_keys(n_row, per_col, features, states, norm_gain, gate_weight, up_weight)
    return tiles(kept, per_col, 1.0 / states.shape[0])


def on_device(states, norm_gain, gate_weight, up_weight):
    n_row = lax.axis_size("row")
    n_col = lax.axis_size("col")
    column = lax.axis_index("col")
    width = gate_weight.shape[1]
    count = states.shape[0]
    wide = states.astype(jnp.float32)
    squares = lax.psum(jnp.sum(wide * wide, axis=1), "col")
    inverse = lax.rsqrt(squares / (states.shape[1] * n_col) + 1e-05)
    normed = (wide * inverse[:, None] * norm_gain[None, :]).astype(jnp.bfloat16)
    gate_part = jnp.dot(normed, gate_weight, preferred_element_type=jnp.float32)
    up_part = jnp.dot(normed, up_weight, preferred_element_type=jnp.float32)
    summed = lax.psum_scatter(
        jnp.concatenate([gate_part, up_part], axis=1), "col", scatter_dimension=0, tiled=True
    )
    own_keys = (jax.nn.silu(summed[:, :width]) * summed[:, width:]).astype(jnp.bfloat16)
    keys = lax.all_gather(own_keys, "col", axis=0, tiled=True)
    per_col = n_row // (2 * n_col)
    scale = 1.0 / count
    partner = keys
    for target in range(1, n_col):
        arrived = passed_along(keys, "row", n_row - target * per_col)
        partner = jnp.where(column == target, arrived, partner)
    tiles = [cross(keys, partner) * scale]
    for offset in range(1, per_col):
        partner = passed_along(partner, "row", n_row - 1)
        tiles.append(cross(keys, partner) * scale)
    opposite = passed_along(keys, "row", n_row // 2)
    near_tiles = jnp.stack(tiles, axis=0)[None]
    slab = width // n_col
    own_cols = lax.dynamic_slice_in_dim(keys, column * slab, slab, 1)
    far_tiles = (cross(own_cols, opposite) * scale)[None]
    return (near_tiles, far_tiles)


def fits(mesh, states, gate_weight):
    n_row, n_col = mesh.shape["row"], mesh.shape["col"]
    width = gate_weight.shape[1] // n_row
    return n_col == 2 and n_row == 8 * n_col and width % (4 * LANES) in (0, 2 * LANES) and width // (2 * LANES) >= SLOTS and states.shape[0] % (2 * LANES) == 0


def solution(mesh):
    placed = (P(None, "col"), P("col"), P("col", "row"), P("col", "row"))

    def program(states, norm_gain, gate_weight, up_weight):
        on_each = by_routes if fits(mesh, states, gate_weight) else on_device
        return jax.shard_map(
            on_each,
            mesh=mesh,
            in_specs=placed,
            out_specs=(P("row", "col", None, None), P("row", "col", None)),
            check_vma=False,
        )(states, norm_gain, gate_weight, up_weight)

    return program
```

```python
import functools

import jax
import jax.numpy as jnp
from jax import lax
from jax.experimental import pallas as pl
from jax.experimental.pallas import tpu as pltpu
from jax.sharding import PartitionSpec as P

LANES = 128
SLOTS = 4
PARTS = 1
CROSS = 8
MESH = pl.DeviceIdType.MESH
(SUM, PAIR, NEXT_OWN, NEXT_OTHER, FAR_OWN, FAR_OTHER, RELAY_OWN, RELAY_OTHER,
 LAST_OWN, LAST_OTHER, SIDE_OWN, SIDE_OTHER, CORE_ODD, CORE_TOP, ACROSS) = range(15)
OWN, STEP, OPPOSITE, BASE1, BASE2, BASE3 = range(6)


def passed_along(shard, axis, by):
    devices = lax.axis_size(axis)
    return lax.ppermute(shard, axis, [(i, (i + by) % devices) for i in range(devices)])


def cross(left, right):
    return lax.dot_general(
        left, right, (((0,), (0,)), ((), ())), preferred_element_type=jnp.float32
    )


def gather_kernel(n_row, step, features, x_hbm, gain_ref, gate_hbm, up_hbm, kept, x_ref, wbuf, partial, sent,
                  got, mine, squares, squares_got, x_sem, w_sem, local_sem, norm_sem, send_sem, recv_sem):
    row = lax.axis_index("row")
    col = lax.axis_index("col")
    core = lax.rem(row, 2)
    y = lax.rem(lax.div(row, 2), 2)
    items, few, wide = sent.shape
    count, depth = x_ref.shape
    strips = squares.shape[0]
    cut = wide // 2
    half = count // 2
    chunks = items // PARTS
    own_rows = pl.ds(pl.multiple_of(col * half, half), half)
    other_rows = pl.ds(pl.multiple_of((1 - col) * half, half), half)
    cross = few * CROSS // 64 * 4

    pair = (row, 1 - col)
    level = lax.div(row, step)
    below = (lax.rem(row + n_row - step, n_row), col)
    above = (lax.rem(row + step, n_row), col)
    two_off = (lax.rem(row + 2 * step, n_row), col)
    side = (row + 2 - 4 * y, col)
    twin = (row + 1 - 2 * core, col)

    def weights(j, slot):
        cols = pl.ds(pl.multiple_of(j * cut, cut), cut)
        return (
            pltpu.make_async_copy(gate_hbm.at[:, cols], wbuf.at[slot, :, pl.ds(0, cut)], w_sem.at[slot, 0]),
            pltpu.make_async_copy(up_hbm.at[:, cols], wbuf.at[slot, :, pl.ds(cut, cut)], w_sem.at[slot, 1]),
        )

    def strip(r):
        return pl.ds(pl.multiple_of(r * LANES, LANES), LANES)

    def states(r):
        return pltpu.make_async_copy(x_hbm.at[strip(r)], x_ref.at[strip(r)], x_sem.at[r])

    def part(slot, i, side=None, skip=0, rows=None):
        start = lax.rem(i, PARTS) * 2 * few
        if side is None:
            rows = 2 * few
        else:
            start = start + side * few + skip
            rows = few if rows is None else rows
        return kept.at[slot, lax.div(i, PARTS), pl.ds(pl.multiple_of(start, 16), rows)]

    def remote(kind, i, src, dst, to):
        return pltpu.make_async_remote_copy(
            src_ref=src, dst_ref=dst, send_sem=send_sem.at[kind, i], recv_sem=recv_sem.at[kind, i],
            device_id=to, device_id_type=MESH,
        )

    def copies(i):
        own = functools.partial(part, i=i, side=col)
        other = functools.partial(part, i=i, side=1 - col)
        fewer = functools.partial(part, i=i, side=1 - col, rows=few - cross)
        crossing = part(OPPOSITE, i, col, few - cross, cross)
        made = {
            SUM: (sent.at[i], got.at[i], pair),
            PAIR: (mine.at[i], own(OWN), pair),
            NEXT_OWN: (mine.at[i], own(STEP), below),
            NEXT_OTHER: (other(OWN), other(STEP), below),
            FAR_OWN: (mine.at[i], own(OPPOSITE), two_off),
            FAR_OTHER: (fewer(OWN), fewer(OPPOSITE), two_off),
            RELAY_OWN: (own(STEP), own(OPPOSITE), below),
            RELAY_OTHER: (fewer(STEP), fewer(OPPOSITE), below),
            LAST_OWN: (own(OPPOSITE), own(STEP), above),
            LAST_OTHER: (other(OPPOSITE), other(STEP), above),
            SIDE_OWN: (own(col + 1 - y), own(BASE2), side),
            SIDE_OTHER: (other(col + 1 - y), other(BASE2), side),
            CORE_ODD: (part(BASE2 * (1 - core) + col * core, i), part(BASE1, i), twin),
            CORE_TOP: (part((col + 1) * (1 - core) + BASE2 * core, i), part(BASE3, i), twin),
            ACROSS: (crossing, crossing, pair),
        }
        return {kind: functools.partial(remote, kind, i, *ends) for kind, ends in made.items()}

    def local(i):
        return pltpu.make_async_copy(mine.at[i], part(OWN, i, col), local_sem.at[i])

    for r in range(strips):
        states(r).start()
    for copy in weights(0, 0):
        copy.start()
    barrier = pltpu.get_barrier_semaphore()
    for device in (pair, below, above, two_off, side, twin):
        pl.semaphore_signal(barrier, inc=1, device_id=device, device_id_type=MESH)

    @pl.loop(0, strips)
    def _(r):
        states(r).wait()
        total = jnp.zeros((LANES, LANES), jnp.float32)
        for g in range(0, depth, LANES):
            v = x_ref[strip(r), g:g + LANES].astype(jnp.float32)
            total += v * v
        squares[r] = jnp.broadcast_to(jnp.sum(total.T, axis=0, keepdims=True), squares.shape[1:])

    pl.semaphore_wait(barrier, 6)
    swap = pltpu.make_async_remote_copy(
        src_ref=squares, dst_ref=squares_got, send_sem=norm_sem.at[0], recv_sem=norm_sem.at[1],
        device_id=pair, device_id_type=MESH,
    )
    swap.start()
    swap.wait()

    @pl.loop(0, strips)
    def _(r):
        total = squares[r] + squares_got[r]
        inverse = lax.rsqrt(jnp.broadcast_to(total[:1], (LANES, LANES)).T / features + 1e-05)
        for g in range(0, depth, LANES):
            v = x_ref[strip(r), g:g + LANES].astype(jnp.float32)
            x_ref[strip(r), g:g + LANES] = (v * inverse * gain_ref[:, g:g + LANES]).astype(jnp.bfloat16)

    def stage(t, lag, act):
        i = t - lag

        @pl.when(jnp.logical_and(i >= 0, i < items))
        def _():
            act(i, copies(i))

    def multiply(i, copy):
        j = lax.div(i, PARTS)
        slot = lax.rem(j, 2)

        @pl.when(lax.rem(i, PARTS) == 0)
        def _():
            for w in weights(j, slot):
                w.wait()

            @pl.when(j + 1 < chunks)
            def _():
                for w in weights(j + 1, 1 - slot):
                    w.start()

            theirs = jnp.dot(
                x_ref[other_rows, :], wbuf[slot], preferred_element_type=jnp.float32
            ).astype(jnp.bfloat16)
            for p in range(PARTS):
                sent[i + p] = theirs[p * few:(p + 1) * few]
            copy[SUM]().start()
            ours = jnp.dot(x_ref[own_rows, :], wbuf[slot], preferred_element_type=jnp.float32)
            for p in range(PARTS):
                partial[slot, p] = ours[p * few:(p + 1) * few]

        pl.when(lax.rem(i, PARTS) > 0)(lambda: copy[SUM]().start())

    def activate(i, copy):
        copy[SUM]().wait_recv()
        total = partial[lax.rem(lax.div(i, PARTS), 2), lax.rem(i, PARTS)] + got[i].astype(jnp.float32)
        gate = total[:, :cut]
        mine[i] = (gate / (1.0 + jnp.exp(-gate)) * total[:, cut:]).astype(jnp.bfloat16)
        copy[PAIR]().start()
        start(copy, FAR_OWN)
        start(copy, NEXT_OWN)
        local(i).start()

    senders = {
        NEXT_OWN: level >= 1, NEXT_OTHER: level >= 1,
        FAR_OWN: level <= 1, FAR_OTHER: level <= 1,
        RELAY_OWN: jnp.logical_or(level == 1, level == 2),
        RELAY_OTHER: jnp.logical_or(level == 1, level == 2),
        LAST_OWN: level == 2, LAST_OTHER: level == 2,
    }
    receivers = {
        NEXT_OWN: level <= 2, NEXT_OTHER: level <= 2,
        FAR_OWN: level >= 2, FAR_OTHER: level >= 2,
        RELAY_OWN: level <= 1, RELAY_OTHER: level <= 1,
        LAST_OWN: level == 3, LAST_OTHER: level == 3,
    }

    def start(copy, kind):
        pl.when(senders[kind])(lambda: copy[kind]().start())

    def receive(copy, kind):
        pl.when(receivers[kind])(lambda: copy[kind]().wait_recv())

    def across(copy, here):
        pl.when(here)(lambda: copy[ACROSS]().start())

    def crossed(copy, here):
        pl.when(here)(lambda: copy[ACROSS]().wait_recv())

    def paired(i, copy):
        copy[PAIR]().wait_recv()
        start(copy, FAR_OTHER)
        start(copy, NEXT_OTHER)

    def hop_own(i, copy):
        receive(copy, NEXT_OWN)
        start(copy, RELAY_OWN)
        receive(copy, FAR_OWN)
        start(copy, LAST_OWN)
        across(copy, level >= 2)

    def hop_other(i, copy):
        receive(copy, NEXT_OTHER)
        start(copy, RELAY_OTHER)

    def onward(i, copy):
        receive(copy, FAR_OTHER)
        crossed(copy, level >= 2)
        start(copy, LAST_OTHER)
        receive(copy, RELAY_OWN)
        across(copy, level <= 1)
        local(i).wait()
        receive(copy, LAST_OWN)
        copy[SIDE_OWN]().start()

    def sideways(i, copy):
        receive(copy, RELAY_OTHER)
        crossed(copy, level <= 1)
        receive(copy, LAST_OTHER)
        copy[SIDE_OTHER]().start()

    def within(i, copy):
        copy[SIDE_OWN]().wait_recv()
        copy[SIDE_OTHER]().wait_recv()
        copy[CORE_ODD]().start()
        copy[CORE_TOP]().start()

    def arrive(i, copy):
        copy[CORE_ODD]().wait_recv()
        copy[CORE_TOP]().wait_recv()
        for kind in copy:
            if kind in senders:
                pl.when(senders[kind])(lambda kind=kind: copy[kind]().wait_send())
            else:
                copy[kind]().wait_send()

    @pl.loop(0, items + 7)
    def _(t):
        stage(t, 0, multiply)
        stage(t, 1, activate)
        stage(t, 2, paired)
        stage(t, 2, hop_own)
        stage(t, 3, hop_other)
        stage(t, 4, onward)
        stage(t, 5, sideways)
        stage(t, 6, within)
        stage(t, 7, arrive)


def gather_keys(n_row, step, features, states, norm_gain, gate_weight, up_weight):
    count, depth = states.shape
    width = gate_weight.shape[1]
    cut = LANES
    items = width // cut * PARTS
    few = count // 2 // PARTS
    strips = count // LANES
    return pl.pallas_call(
        functools.partial(gather_kernel, n_row, step, features),
        out_shape=jax.ShapeDtypeStruct((6, width // LANES, count, LANES), jnp.bfloat16),
        in_specs=[
            pl.BlockSpec(memory_space=pl.ANY),
            pl.BlockSpec(memory_space=pltpu.VMEM),
            pl.BlockSpec(memory_space=pl.ANY),
            pl.BlockSpec(memory_space=pl.ANY),
        ],
        out_specs=pl.BlockSpec(memory_space=pl.ANY),
        scratch_shapes=[
            pltpu.VMEM((count, depth), jnp.bfloat16),
            pltpu.VMEM((2, depth, 2 * cut), jnp.bfloat16),
            pltpu.VMEM((2, PARTS, few, 2 * cut), jnp.float32),
            pltpu.VMEM((items, few, 2 * cut), jnp.bfloat16),
            pltpu.VMEM((items, few, 2 * cut), jnp.bfloat16),
            pltpu.VMEM((items, few, LANES), jnp.bfloat16),
            pltpu.VMEM((strips, 8, LANES), jnp.float32),
            pltpu.VMEM((strips, 8, LANES), jnp.float32),
            pltpu.SemaphoreType.DMA((strips,)),
            pltpu.SemaphoreType.DMA((2, 2)),
            pltpu.SemaphoreType.DMA((items,)),
            pltpu.SemaphoreType.DMA((2,)),
            pltpu.SemaphoreType.DMA((15, items)),
            pltpu.SemaphoreType.DMA((15, items)),
        ],
        compiler_params=pltpu.CompilerParams(
            collective_id=0, has_side_effects=True, vmem_limit_bytes=56 * 2**20
        ),
        name="gather_keys",
    )(states, norm_gain.reshape(1, depth), gate_weight, up_weight)


def tiles_kernel(scale, kept, near_hbm, far_hbm, left, turned, right, filled, left_sem, right_sem, out_sem):
    col = lax.axis_index("col")
    blocks, count = left.shape[0], left.shape[1]
    slab = far_hbm.shape[1]
    per_col = near_hbm.shape[1]
    pairs = blocks // 2
    pair = 2 * LANES
    slots = filled.shape[0]
    nears = per_col * pairs

    def fetch(m):
        block = jnp.where(m == 0, col, jnp.where(m == per_col, OPPOSITE, OPPOSITE + m))
        slot = lax.rem(m, 2)
        return pltpu.make_async_copy(kept.at[block], right.at[slot], right_sem.at[slot])

    def near_out(n):
        slot = lax.rem(n, slots)
        cols = pl.ds(pl.multiple_of(lax.rem(n, pairs) * pair, pair), pair)
        return pltpu.make_async_copy(filled.at[slot], near_hbm.at[0, lax.div(n, pairs), :, cols], out_sem.at[slot])

    def far_out(n):
        slot = lax.rem(n, slots)
        cols = pl.ds(pl.multiple_of((n - nears) * pair, pair), pair)
        return pltpu.make_async_copy(filled.at[slot, pl.ds(0, slab)], far_hbm.at[0, :, cols], out_sem.at[slot])

    def product(lefts, m, b):
        slot = lax.rem(m, 2)
        both = jnp.concatenate([right[slot, 2 * b], right[slot, 2 * b + 1]], axis=1)
        return jnp.dot(lefts, both, preferred_element_type=jnp.float32) * scale

    own = [pltpu.make_async_copy(kept.at[OWN, k], left.at[k], left_sem.at[k]) for k in range(blocks)]
    for piece in own:
        piece.start()
    fetch(0).start()
    for k in range(blocks):
        own[k].wait()
        turned[k * LANES:(k + 1) * LANES, :] = left[k].T

    @pl.loop(0, nears)
    def _(n):
        m, b = lax.div(n, pairs), lax.rem(n, pairs)

        @pl.when(b == 0)
        def _():
            fetch(m).wait()
            fetch(m + 1).start()

        pl.when(n >= slots)(lambda: near_out(n - slots).wait())
        filled[lax.rem(n, slots)] = product(turned[...], m, b)
        near_out(n).start()

    fetch(per_col).wait()

    @pl.loop(nears, nears + pairs)
    def _(n):
        pl.when(n - slots < nears)(lambda: near_out(n - slots).wait())
        pl.when(n - slots >= nears)(lambda: far_out(n - slots).wait())
        lefts = turned[pl.ds(pl.multiple_of(col * slab, LANES), slab), :]
        filled[lax.rem(n, slots), :slab] = product(lefts, per_col, n - nears)
        far_out(n).start()

    for n in range(nears + pairs - slots, nears + pairs):
        far_out(n).wait()


def tiles(kept, per_col, scale):
    _, blocks, count, _ = kept.shape
    width = blocks * LANES
    slab = width // 2
    return pl.pallas_call(
        functools.partial(tiles_kernel, scale),
        in_specs=[pl.BlockSpec(memory_space=pl.ANY)],
        out_specs=[pl.BlockSpec(memory_space=pl.ANY), pl.BlockSpec(memory_space=pl.ANY)],
        out_shape=(
            jax.ShapeDtypeStruct((1, per_col, width, width), jnp.float32),
            jax.ShapeDtypeStruct((1, slab, width), jnp.float32),
        ),
        scratch_shapes=[
            pltpu.VMEM((blocks, count, LANES), jnp.bfloat16),
            pltpu.VMEM((width, count), jnp.bfloat16),
            pltpu.VMEM((2, blocks, count, LANES), jnp.bfloat16),
            pltpu.VMEM((SLOTS, width, 2 * LANES), jnp.float32),
            pltpu.SemaphoreType.DMA((blocks,)),
            pltpu.SemaphoreType.DMA((2,)),
            pltpu.SemaphoreType.DMA((SLOTS,)),
        ],
        compiler_params=pltpu.CompilerParams(vmem_limit_bytes=56 * 2**20),
        name="tiles",
    )(kept)


def by_routes(states, norm_gain, gate_weight, up_weight):
    n_row = lax.axis_size("row")
    n_col = lax.axis_size("col")
    per_col = n_row // (2 * n_col)
    features = states.shape[1] * n_col
    kept = gather_keys(n_row, per_col, features, states, norm_gain, gate_weight, up_weight)
    return tiles(kept, per_col, 1.0 / states.shape[0])


def on_device(states, norm_gain, gate_weight, up_weight):
    n_row = lax.axis_size("row")
    n_col = lax.axis_size("col")
    column = lax.axis_index("col")
    width = gate_weight.shape[1]
    count = states.shape[0]
    wide = states.astype(jnp.float32)
    squares = lax.psum(jnp.sum(wide * wide, axis=1), "col")
    inverse = lax.rsqrt(squares / (states.shape[1] * n_col) + 1e-05)
    normed = (wide * inverse[:, None] * norm_gain[None, :]).astype(jnp.bfloat16)
    gate_part = jnp.dot(normed, gate_weight, preferred_element_type=jnp.float32)
    up_part = jnp.dot(normed, up_weight, preferred_element_type=jnp.float32)
    summed = lax.psum_scatter(
        jnp.concatenate([gate_part, up_part], axis=1), "col", scatter_dimension=0, tiled=True
    )
    own_keys = (jax.nn.silu(summed[:, :width]) * summed[:, width:]).astype(jnp.bfloat16)
    keys = lax.all_gather(own_keys, "col", axis=0, tiled=True)
    per_col = n_row // (2 * n_col)
    scale = 1.0 / count
    partner = keys
    for target in range(1, n_col):
        arrived = passed_along(keys, "row", n_row - target * per_col)
        partner = jnp.where(column == target, arrived, partner)
    tiles = [cross(keys, partner) * scale]
    for offset in range(1, per_col):
        partner = passed_along(partner, "row", n_row - 1)
        tiles.append(cross(keys, partner) * scale)
    opposite = passed_along(keys, "row", n_row // 2)
    near_tiles = jnp.stack(tiles, axis=0)[None]
    slab = width // n_col
    own_cols = lax.dynamic_slice_in_dim(keys, column * slab, slab, 1)
    far_tiles = (cross(own_cols, opposite) * scale)[None]
    return (near_tiles, far_tiles)


def fits(mesh, states, gate_weight):
    n_row, n_col = mesh.shape["row"], mesh.shape["col"]
    width = gate_weight.shape[1] // n_row
    return n_col == 2 and n_row == 8 * n_col and width % (4 * LANES) in (0, 2 * LANES) and width // (2 * LANES) >= SLOTS and states.shape[0] % (2 * LANES) == 0


def solution(mesh):
    placed = (P(None, "col"), P("col"), P("col", "row"), P("col", "row"))

    def program(states, norm_gain, gate_weight, up_weight):
        on_each = by_routes if fits(mesh, states, gate_weight) else on_device
        return jax.shard_map(
            on_each,
            mesh=mesh,
            in_specs=placed,
            out_specs=(P("row", "col", None, None), P("row", "col", None)),
            check_vma=False,
        )(states, norm_gain, gate_weight, up_weight)

    return program
```
